1024 devices in a mesh: dp: 64 (over z_hi, y, core), tensor: 16 (over x, z_lo).
Axes of the slice: x: 8, y: 8, z: 8 (z_hi: 4, z_lo: 2; z = z_hi * 2 + z_lo), core: 2. Of those that a mesh axis runs over, the one named last changes fastest.
Arguments:
- activations: bfloat16 [131072, 4096], P(('dp', 'tensor')), may hold values from -24 to 24
- value_weight: bfloat16 [4096, 512], P('tensor'), may hold values from -0.09375 to 0.09375
- value_cotangent: bfloat16 [131072, 512], P(('dp', 'tensor')), may hold values from -6 to 6
Outputs:
- value_proj: bfloat16 [131072, 512], P(('dp', 'tensor'))
- input_grad: bfloat16 [131072, 4096], P(('dp', 'tensor'))
- weight_grad: float32 [4096, 512], P(('tensor', 'dp'))
The draws below stay inside these ranges and needn't reach their ends.
All inputs are finite; a program needn't handle non-finite values.
Results may differ from the reference program's by a relative error of at most 0.001.
Values may be sent and summed in bfloat16 or wider, within the bound.
A program may use at most 32 MiB of HBM per device.

```python
import jax
import jax.numpy as jnp

D = 4096
VDIM = 512
TOKENS = 131072


def with_spikes(result, stream_key, source, target, blocks, factor):
    owner, partner = [(jnp.arange(result.shape[dim]) // (result.shape[dim] // blocks)).reshape([-1 if axis == dim else 1 for axis in range(result.ndim)]) for dim in (source, target)]
    chosen = jax.random.permutation(stream_key, blocks)[partner]
    strong = (owner == chosen) | (owner == (partner + blocks // 2) % blocks)
    return jnp.where(strong, factor * result, result)


def block_scale(stream_key, shape, split, low, top_value):
    def one(dim, parts):
        steps = jax.random.uniform(jax.random.fold_in(jax.random.fold_in(stream_key, 6), dim), (parts,), jnp.float32, low / len(split), top_value / len(split))
        return jnp.repeat(jnp.exp(steps), shape[dim] // parts).reshape((-1,) + (1,) * (len(shape) - dim - 1))

    gain = one(*split[0])
    for cut in split[1:]:
        gain = gain * one(*cut)
    return gain


def centred(key, shape, scale, most, cuts=(), held_as=jnp.bfloat16):
    drawn = scale * jax.random.normal(key, shape, jnp.float32)
    if cuts:
        drawn = drawn * block_scale(key, shape, cuts, -0.22, 0.18)
    return jnp.clip(drawn, -most, most).astype(held_as)


def gaussian_with(own_key, dims, scale, bound, split, heavy, dtype=jnp.bfloat16):
    result = scale * jax.random.normal(own_key, dims, jnp.float32)
    if split:
        result = result * block_scale(own_key, dims, split, -0.22, 0.18)
    return jnp.clip(with_spikes(result, jax.random.fold_in(own_key, 3), *heavy), -bound, bound).astype(dtype)


def setup_inputs(seed: int = 0) -> dict:
    streams_of = jax.random.split(jax.random.key(seed), 4)
    return {
        "activations": gaussian_with(streams_of[0], (TOKENS, D), 1.0, 24.0, ((0, 1024),), (0, 1, 1024, 6.0)),
        "value_weight": centred(streams_of[1], (D, VDIM), D ** -0.5, 0.09375, ((0, 16),)),
        "value_cotangent": centred(streams_of[2], (TOKENS, VDIM), 1.0, 6.0, ((0, 1024),)),
    }


def reference(activations, value_weight, value_cotangent):
    value_proj = jnp.dot(activations, value_weight, preferred_element_type=jnp.float32).astype(jnp.bfloat16)
    input_grad = jnp.dot(value_cotangent, value_weight.T, preferred_element_type=jnp.float32).astype(jnp.bfloat16)
    total = jnp.dot(activations.T, value_cotangent, preferred_element_type=jnp.float32)
    weight_grad = total / jnp.sqrt(jnp.float32(TOKENS))
    return (value_proj, input_grad, weight_grad)
```

```python
import functools

import jax
import jax.numpy as jnp
from jax import lax
from jax.experimental import pallas as pl
from jax.experimental.pallas import tpu as pltpu
from jax.sharding import PartitionSpec as P

MESH = pl.DeviceIdType.MESH
RING = 8
ITEMS = 28


def _mod(v):
    return lax.rem(v + 4 * RING, RING)


def _kernel(scale, acts, w, cot, vp_out, ig_out, wg_out,
            a_all, c_pair, c_own, w_all, part, recv_r, recv_l, recv2_r, recv2_l, recv3_r, recv3_l,
            vp_acc, vp_buf, ig_buf, fin, fin_in, wg_buf,
            s_load, s_ax, r_ax, s_cx, r_cx, s_zx, r_zx,
            s_r, r_r, s_l, r_l, s_x, r_x, s_p, r_p,
            s2_r, r2_r, s2_l, r2_l, s3_r, r3_r, s3_l, r3_l, s_f, r_f, s_out):
    dp, tn = lax.axis_index("dp"), lax.axis_index("tensor")
    c, y, zh = lax.rem(dp, 2), lax.rem(lax.div(dp, 2), RING), lax.div(dp, 2 * RING)
    x, zl = lax.div(tn, 2), lax.rem(tn, 2)
    z = zh * 2 + zl
    oc = 1 - c
    sx = 1 - 2 * c
    pa = y * oc + z * c
    pb = z * oc + y * c

    def dev(xx, yy, zz, cc):
        return {"dp": lax.div(zz, 2) * (2 * RING) + yy * 2 + cc, "tensor": xx * 2 + lax.rem(zz, 2)}

    def along_a(step):
        return dev(x, _mod(y + step * oc), _mod(z + step * c), c)

    def along_b(step):
        return dev(x, _mod(y + step * c), _mod(z + step * oc), c)

    def along_x(step):
        return dev(_mod(x + step), y, z, c)

    partner = dev(x, y, z, oc)
    tok, cols = 128, 512

    loads = [
        pltpu.make_async_copy(acts, a_all.at[pl.ds(0, tok)], s_load.at[0]),
        pltpu.make_async_copy(cot.at[:, pl.ds(pl.multiple_of(c * 256, 256), 256)], c_pair.at[pl.ds(0, tok)], s_load.at[1]),
        pltpu.make_async_copy(cot, c_own, s_load.at[2]),
        pltpu.make_async_copy(w, w_all.at[x, pl.ds(zl * 4, 4)], s_load.at[3]),
    ]
    for load in loads:
        load.start()

    barrier = pltpu.get_barrier_semaphore()
    for there in (partner, along_a(1), along_a(-1), along_b(1), along_b(-1), along_x(1), along_x(-1)):
        pl.semaphore_signal(barrier, inc=1, device_id=there, device_id_type=MESH)
    pl.semaphore_wait(barrier, 7)

    def remote(src, dst, send, recv, there):
        return pltpu.make_async_remote_copy(
            src_ref=src, dst_ref=dst, send_sem=send, recv_sem=recv, device_id=there, device_id_type=MESH
        )

    def order(j):
        k = j // 2
        return 4 - k if j % 2 == 0 else k - 3

    def a_copy(j):
        block = pl.ds(pl.multiple_of(_mod(x + order(j)) * cols, cols), cols)
        return remote(acts.at[:, block], a_all.at[pl.ds(tok, tok), block], s_ax.at[j], r_ax.at[j], partner)

    c_copy = remote(cot.at[:, pl.ds(pl.multiple_of(oc * 256, 256), 256)], c_pair.at[pl.ds(tok, tok)], s_cx, r_cx, partner)
    c_copy.start()
    for j in range(8):
        a_copy(j).start()

    def unit(m):
        return lax.rem(zl + m // 4, 2) * 4 + lax.rem(m, 4)

    z_there = dev(x, y, _mod(z - sx), c)
    z_copy = remote(w, w_all.at[x, pl.ds(zl * 4, 4)], s_zx, r_zx, z_there)
    z_copy.start()
    z_wait = remote(w, w_all.at[x, pl.ds((1 - zl) * 4, 4)], s_zx, r_zx, z_there)

    x_there = along_x(sx)

    def x_place(i, m):
        return w_all.at[_mod(x - sx * (i // 8 + 1)), unit(m)]

    def x_in(i):
        m = lax.rem(i, 8) + lax.div(i, 24) * 4 * c
        return x_place(i, m)

    def x_recv(i):
        here = x_in(i)
        remote(here, here, s_x.at[i], r_x.at[i], x_there).wait_recv()
        remote(here, here, s_p.at[i], r_p.at[i], partner).start()

    def x_send(i, out):
        here = x_in(i)
        remote(here, here, s_x.at[out], r_x.at[out], x_there).start()

    def p_recv(i):
        m = lax.rem(i, 8) + lax.div(i, 24) * 4 * oc
        here = w_all.at[_mod(x + sx * (i // 8 + 1)), unit(m)]
        remote(here, here, s_p.at[i], r_p.at[i], partner).wait_recv()

    for m in range(4):
        here = w_all.at[x, unit(m)]
        remote(w.at[m], here, s_x.at[m], r_x.at[m], x_there).start()

    def weights_block(block, first=False):
        at = pl.ds(pl.multiple_of(block * cols, cols), cols)
        wb = w_all[block].reshape(cols, cols)
        term = jnp.dot(a_all[pl.ds(0, tok), at], wb, preferred_element_type=jnp.float32)
        if first:
            vp_acc[...] = term
        else:
            vp_acc[...] += term
        grad = lax.dot_general(c_own[...], wb, (((1,), (1,)), ((), ())), preferred_element_type=jnp.float32)
        ig_buf[:, at] = grad.astype(jnp.bfloat16)
        pltpu.make_async_copy(ig_buf.at[:, at], ig_out.at[:, at], s_out.at[block]).start()

    right, left = along_a(1), along_a(-1)

    def r_copy(n, to, xx):
        return remote(part.at[_mod(pa + to), _mod(x + xx)], recv_r.at[n], s_r.at[n], r_r.at[n], right)

    def l_copy(n, to, xx):
        return remote(part.at[_mod(pa - to), _mod(x + xx)], recv_l.at[n], s_l.at[n], r_l.at[n], left)

    for load in loads[:3]:
        load.wait()
    c_copy.wait_recv()
    for j in range(8):
        k = j // 2
        a_copy(j).wait_recv()
        xb = _mod(x + order(j))
        at = pl.ds(pl.multiple_of(xb * cols, cols), cols)
        prod = lax.dot_general(
            a_all[:, at], c_pair[...], (((0,), (0,)), ((), ())), preferred_element_type=jnp.float32
        )
        for zz in range(8):
            base = (zz % 2) * 256 + (zz // 2) * 64
            for yy in range(8):
                part[yy * oc + zz * c, xb, zz * oc + yy * c] = prod[base + yy * 8 : base + yy * 8 + 8]
        if j % 2 == 0:
            r_copy(2 * k, 4, order(j)).start()
            l_copy(2 * k + 1, 3, order(j)).start()
        else:
            r_copy(2 * k + 1, 3, order(j)).start()
            l_copy(2 * k, 4, order(j)).start()

    loads[3].wait()
    z_wait.wait_recv()
    for m in range(4, 8):
        here = w_all.at[x, unit(m)]
        remote(here, here, s_x.at[m], r_x.at[m], x_there).start()
    weights_block(x, first=True)

    def pass_on(i, n_out):
        x_recv(i)
        x_send(i, n_out)

    lax.fori_loop(0, 8, lambda i, u: (pass_on(i, i + 8), u)[1], 0)

    def ring_step(p, k):
        n_even, n_odd = 8 * (p - 1) + 2 * k, 8 * (p - 1) + 2 * k + 1
        e_r, e_l = 4 - k, k - 3
        r_copy(n_even, 0, 0).wait_recv()
        part[_mod(pa + 4 - p), _mod(x + e_r)] += recv_r[n_even]
        l_copy(n_even, 0, 0).wait_recv()
        part[_mod(pa - 4 + p), _mod(x + e_l)] += recv_l[n_even]
        r_copy(n_odd, 0, 0).wait_recv()
        part[_mod(pa + 3 - p), _mod(x + e_l)] += recv_r[n_odd]
        l_copy(n_odd, 0, 0).wait_recv()
        part[_mod(pa - 3 + p), _mod(x + e_r)] += recv_l[n_odd]
        if p < 3:
            r_copy(8 * p + 2 * k, 4 - p, e_r).start()
            l_copy(8 * p + 2 * k, 4 - p, e_l).start()
            r_copy(8 * p + 2 * k + 1, 3 - p, e_l).start()
            l_copy(8 * p + 2 * k + 1, 3 - p, e_r).start()
        else:
            r_copy(24 + k, 1, e_r).start()
            l_copy(24 + k, 1, e_l).start()

    def p_block(p):
        lax.fori_loop(8 * p - 8, 8 * p, lambda i, u: (p_recv(i), u)[1], 0)
        weights_block(_mod(x + sx * p))

    for p in (1, 2, 3):

        def tick(k, u, p=p):
            ring_step(p, k)
            for h in range(2):
                i = 8 * p + 2 * k + h
                if p == 1:
                    pass_on(i, i + 8)
                elif p == 2:
                    x_recv(i)

                    @pl.when((1 - lax.div(k, 2)) * oc + lax.div(k, 2) * c == 1)
                    def _():
                        x_send(i, 24 + lax.rem(i, 4))
            if p == 3:
                x_recv(24 + k)
            return u

        lax.fori_loop(0, 2, tick, 0)
        weights_block(_mod(x - sx * p))
        lax.fori_loop(2, 4, tick, 0)
        p_block(p)

    x_right, x_left = along_x(1), along_x(-1)

    def half2(ref, h):
        return ref.at[pl.ds(h * 4, 4)]

    def r2_copy(n):
        src = half2(part.at[pa, _mod(x + 4 - (n + 1) // 2)], n % 2)
        return remote(src, recv2_r.at[n], s2_r.at[n], r2_r.at[n], x_right)

    def l2_copy(n):
        src = half2(part.at[pa, _mod(x - 4 + (n + 1) // 2)], (n + 1) % 2)
        return remote(src, recv2_l.at[n], s2_l.at[n], r2_l.at[n], x_left)

    for k in range(4):
        r_copy(24 + k, 0, 0).wait_recv()
        part[pa, _mod(x + 4 - k)] += recv_r[24 + k]
        l_copy(24 + k, 0, 0).wait_recv()
        part[pa, _mod(x + k - 3)] += recv_l[24 + k]
        if k < 2:
            r2_copy(k).start()
            l2_copy(k).start()

    def last_block():
        lax.fori_loop(24, 28, lambda i, u: (p_recv(i), u)[1], 0)
        weights_block(_mod(x + 4))
        vp_buf[...] = vp_acc[...].astype(jnp.bfloat16)
        pltpu.make_async_copy(vp_buf, vp_out, s_out.at[8]).start()

    last_block()
    for n in range(7):
        to = 4 - (n + 1) // 2 - 1
        r2_copy(n).wait_recv()
        mine = half2(part.at[pa, _mod(x + to)], n % 2)
        mine[...] += recv2_r[n]
        l2_copy(n).wait_recv()
        mine = half2(part.at[pa, _mod(x - to)], (n + 1) % 2)
        mine[...] += recv2_l[n]
        if n + 2 < 7:
            r2_copy(n + 2).start()
            l2_copy(n + 2).start()

    b_right, b_left = along_b(1), along_b(-1)

    def r3_copy(n):
        return remote(part.at[pa, x, _mod(pb + 4 - n)], recv3_r.at[n], s3_r.at[n], r3_r.at[n], b_right)

    def l3_copy(n):
        return remote(part.at[pa, x, _mod(pb - 3 + n)], recv3_l.at[n], s3_l.at[n], r3_l.at[n], b_left)

    r3_copy(0).start()
    l3_copy(0).start()
    for n in range(4):
        if n < 3:
            l3_copy(n).wait_recv()
            part[pa, x, _mod(pb - 2 + n)] += recv3_l[n]
        if n < 2:
            l3_copy(n + 1).start()
        r3_copy(n).wait_recv()
        part[pa, x, _mod(pb + 3 - n)] += recv3_r[n]
        if n < 3:
            r3_copy(n + 1).start()

    total = part[pa, x, pb] / scale
    fin[...] = jnp.where(c == 0, total[4:], total[:4])
    f_copy = remote(fin, fin_in, s_f, r_f, partner)
    f_copy.start()
    stay = jnp.where(c == 0, total[:4], total[4:])
    f_copy.wait_recv()
    other = fin_in[...]
    wg_buf[:, :256] = jnp.where(c == 0, stay, other)
    wg_buf[:, 256:] = jnp.where(c == 0, other, stay)
    wg_copy = pltpu.make_async_copy(wg_buf, wg_out, s_out.at[9])
    wg_copy.start()

    c_copy.wait_send()
    z_copy.wait_send()
    f_copy.wait_send()
    for j in range(8):
        a_copy(j).wait_send()

    def sent(n, u):
        r_copy(n, 0, 0).wait_send()
        l_copy(n, 0, 0).wait_send()
        here = w_all.at[0, 0]
        remote(here, here, s_x.at[n], r_x.at[n], x_there).wait_send()
        remote(here, here, s_p.at[n], r_p.at[n], partner).wait_send()
        return u

    lax.fori_loop(0, ITEMS, sent, 0)
    for n in range(7):
        r2_copy(n).wait_send()
        l2_copy(n).wait_send()
    for n in range(4):
        r3_copy(n).wait_send()
    for n in range(3):
        l3_copy(n).wait_send()
    for b in range(8):
        at = pl.ds(b * cols, cols)
        pltpu.make_async_copy(ig_buf.at[:, at], ig_out.at[:, at], s_out.at[b]).wait()
    pltpu.make_async_copy(vp_buf, vp_out, s_out.at[8]).wait()
    wg_copy.wait()


def per_device(activations, value_weight, value_cotangent):
    tok, d = activations.shape
    rows, v = value_weight.shape
    tokens = tok * lax.axis_size("dp") * lax.axis_size("tensor")
    f32, bf16 = jnp.float32, jnp.bfloat16
    dma, vm = pltpu.SemaphoreType.DMA, pltpu.VMEM
    hbm = pl.BlockSpec(memory_space=pl.ANY)
    return pl.pallas_call(
        functools.partial(_kernel, float(tokens) ** 0.5),
        out_shape=(
            jax.ShapeDtypeStruct((tok, v), bf16),
            jax.ShapeDtypeStruct((tok, d), bf16),
            jax.ShapeDtypeStruct((rows * lax.axis_size("tensor") // 1024, v), f32),
        ),
        in_specs=[hbm] * 3,
        out_specs=(hbm,) * 3,
        scratch_shapes=[
            vm((256, 4096), bf16), vm((256, 256), bf16), vm((128, 512), bf16), vm((8, 8, 64, 512), bf16),
            vm((8, 8, 8, 8, 256), f32), vm((ITEMS, 8, 8, 256), f32), vm((ITEMS, 8, 8, 256), f32),
            vm((7, 4, 8, 256), f32), vm((7, 4, 8, 256), f32), vm((4, 8, 256), f32), vm((3, 8, 256), f32),
            vm((128, 512), f32), vm((128, 512), bf16), vm((128, 4096), bf16),
            vm((4, 256), f32), vm((4, 256), f32), vm((4, 512), f32),
            dma((4,)), dma((8,)), dma((8,)), dma, dma, dma, dma,
            dma((ITEMS,)), dma((ITEMS,)), dma((ITEMS,)), dma((ITEMS,)),
            dma((ITEMS,)), dma((ITEMS,)), dma((ITEMS,)), dma((ITEMS,)),
            dma((7,)), dma((7,)), dma((7,)), dma((7,)), dma((4,)), dma((4,)), dma((3,)), dma((3,)),
            dma, dma, dma((10,)),
        ],
        compiler_params=pltpu.CompilerParams(
            collective_id=0, has_side_effects=True, vmem_limit_bytes=48 * 1024 * 1024
        ),
    )(activations, value_weight.reshape(4, 64, v), value_cotangent)


def solution(mesh):
    placed = (P(("dp", "tensor"), None), P("tensor", None), P(("dp", "tensor"), None))
    return jax.shard_map(
        per_device,
        mesh=mesh,
        in_specs=placed,
        out_specs=(P(("dp", "tensor"), None), P(("dp", "tensor"), None), P(("tensor", "dp"), None)),
        check_vma=False,
    )
```

```python
import functools

import jax
import jax.numpy as jnp
from jax import lax
from jax.experimental import pallas as pl
from jax.experimental.pallas import tpu as pltpu
from jax.sharding import PartitionSpec as P

MESH = pl.DeviceIdType.MESH
RING = 8
ITEMS = 28


def _mod(v):
    return lax.rem(v + 4 * RING, RING)


def _kernel(scale, acts, w, cot, vp_out, ig_out, wg_out,
            a_all, c_pair, c_own, w_all, part, recv_r, recv_l, recv2, s2_buf, recv3,
            vp_acc, vp_buf, ig_buf, wg_buf,
            s_load, s_ax, r_ax, s_cx, r_cx, s_zx, r_zx, s_zp, r_zp,
            s_r, r_r, s_l, r_l, s_x, r_x, s_p, r_p, s_2, r_2, s_3, r_3, s_out):
    dp, tn = lax.axis_index("dp"), lax.axis_index("tensor")
    c, y, zh = lax.rem(dp, 2), lax.rem(lax.div(dp, 2), RING), lax.div(dp, 2 * RING)
    x, zl = lax.div(tn, 2), lax.rem(tn, 2)
    z = zh * 2 + zl
    oc = 1 - c
    sx = 1 - 2 * c
    pa = y * oc + z * c
    pb = z * oc + y * c

    def dev(xx, yy, zz, cc):
        return {"dp": lax.div(zz, 2) * (2 * RING) + yy * 2 + cc, "tensor": xx * 2 + lax.rem(zz, 2)}

    def along_a(step):
        return dev(x, _mod(y + step * oc), _mod(z + step * c), c)

    def along_b(step):
        return dev(x, _mod(y + step * c), _mod(z + step * oc), c)

    def along_x(step):
        return dev(_mod(x + step), y, z, c)

    partner = dev(x, y, z, oc)
    tok, cols = 128, 512

    barrier = pltpu.get_barrier_semaphore()
    for there in (partner, along_a(1), along_a(-1), along_b(1), along_b(-1), along_x(1), along_x(-1)):
        pl.semaphore_signal(barrier, inc=1, device_id=there, device_id_type=MESH)

    loads = [
        pltpu.make_async_copy(acts, a_all.at[pl.ds(0, tok)], s_load.at[0]),
        pltpu.make_async_copy(cot.at[:, pl.ds(pl.multiple_of(c * 256, 256), 256)], c_pair.at[pl.ds(0, tok)], s_load.at[1]),
        pltpu.make_async_copy(cot, c_own, s_load.at[2]),
        pltpu.make_async_copy(w, w_all.at[x, pl.ds(zl * 4, 4)], s_load.at[3]),
    ]
    for load in loads:
        load.start()
    pl.semaphore_wait(barrier, 7)

    def remote(src, dst, send, recv, there):
        return pltpu.make_async_remote_copy(
            src_ref=src, dst_ref=dst, send_sem=send, recv_sem=recv, device_id=there, device_id_type=MESH
        )

    z_there = dev(x, y, _mod(z - sx), c)
    z_copy = remote(w.at[pl.ds(2 * c, 2)], w_all.at[x, pl.ds(zl * 4 + 2 * c, 2)], s_zx, r_zx, z_there)
    z_copy.start()
    z_mine = w_all.at[x, pl.ds((1 - zl) * 4 + 2 * c, 2)]
    z_other = w_all.at[x, pl.ds((1 - zl) * 4 + 2 * oc, 2)]

    def order(j):
        k = j // 2
        return 4 - k if j % 2 == 0 else k - 3

    def a_copy(j):
        block = pl.ds(pl.multiple_of(_mod(x + order(j)) * cols, cols), cols)
        return remote(acts.at[:, block], a_all.at[pl.ds(tok, tok), block], s_ax, r_ax.at[j], partner)

    c_copy = remote(cot.at[:, pl.ds(pl.multiple_of(oc * 256, 256), 256)], c_pair.at[pl.ds(tok, tok)], s_cx, r_cx, partner)
    c_copy.start()
    for j in range(8):
        a_copy(j).start()

    def unit(m):
        return lax.rem(zl + m // 4, 2) * 4 + lax.rem(m, 4)

    x_there = along_x(sx)

    def x_in(i):
        m = lax.rem(i, 8) + lax.div(i, 24) * 4 * c
        return w_all.at[_mod(x - sx * (i // 8 + 1)), unit(m)]

    def x_recv(i):
        here = x_in(i)
        remote(here, here, s_x, r_x.at[i], x_there).wait_recv()
        remote(here, here, s_p, r_p.at[i // 8], partner).start()

    def x_send(i, out):
        here = x_in(i)
        remote(here, here, s_x, r_x.at[out], x_there).start()

    def x_own(m):
        here = w_all.at[x, unit(m)]
        remote(here, here, s_x, r_x.at[m], x_there).start()

    for m in range(4):
        remote(w.at[m], w_all.at[x, unit(m)], s_x, r_x.at[m], x_there).start()

    def weights_block(block, first=False):
        at = pl.ds(pl.multiple_of(block * cols, cols), cols)
        wb = w_all[block].reshape(cols, cols)
        term = jnp.dot(a_all[pl.ds(0, tok), at], wb, preferred_element_type=jnp.float32)
        if first:
            vp_acc[...] = term
        else:
            vp_acc[...] += term
        grad = lax.dot_general(c_own[...], wb, (((1,), (1,)), ((), ())), preferred_element_type=jnp.float32)
        ig_buf[:, at] = grad.astype(jnp.bfloat16)
        pltpu.make_async_copy(ig_buf.at[:, at], ig_out.at[:, at], s_out.at[block]).start()

    def partner_block(p):
        whole = w_all.at[0] if p < 4 else w_all.at[0, pl.ds(0, 4)]
        remote(whole, whole, s_p, r_p.at[p - 1], partner).wait_recv()
        if p < 4:
            weights_block(_mod(x + sx * p))

    right, left = along_a(1), along_a(-1)

    def r_copy(n, to, xx):
        return remote(part.at[_mod(pa + to), _mod(x + xx)], recv_r.at[n], s_r, r_r.at[n], right)

    def l_copy(n, to, xx):
        return remote(part.at[_mod(pa - to), _mod(x + xx)], recv_l.at[n], s_l, r_l.at[n], left)

    for load in loads[:3]:
        load.wait()
    c_copy.wait_recv()
    for j in range(8):
        k = j // 2
        a_copy(j).wait_recv()
        xb = _mod(x + order(j))
        at = pl.ds(pl.multiple_of(xb * cols, cols), cols)
        prod = lax.dot_general(
            a_all[:, at], c_pair[...], (((0,), (0,)), ((), ())), preferred_element_type=jnp.float32
        )
        for zz in range(8):
            base = (zz % 2) * 256 + (zz // 2) * 64
            for yy in range(8):
                part[yy * oc + zz * c, xb, zz * oc + yy * c] = prod[base + yy * 8 : base + yy * 8 + 8]
        if j % 2 == 0:
            r_copy(2 * k, 4, order(j)).start()
            l_copy(2 * k + 1, 3, order(j)).start()
        else:
            r_copy(2 * k + 1, 3, order(j)).start()
            l_copy(2 * k, 4, order(j)).start()

    def ring_step(p, k):
        n_even, n_odd = 8 * (p - 1) + 2 * k, 8 * (p - 1) + 2 * k + 1
        e_r, e_l = 4 - k, k - 3
        r_copy(n_even, 0, 0).wait_recv()
        part[_mod(pa + 4 - p), _mod(x + e_r)] += recv_r[n_even]
        l_copy(n_even, 0, 0).wait_recv()
        part[_mod(pa - 4 + p), _mod(x + e_l)] += recv_l[n_even]
        r_copy(n_odd, 0, 0).wait_recv()
        part[_mod(pa + 3 - p), _mod(x + e_l)] += recv_r[n_odd]
        l_copy(n_odd, 0, 0).wait_recv()
        part[_mod(pa - 3 + p), _mod(x + e_r)] += recv_l[n_odd]
        if p < 3:
            r_copy(8 * p + 2 * k, 4 - p, e_r).start()
            l_copy(8 * p + 2 * k, 4 - p, e_l).start()
            r_copy(8 * p + 2 * k + 1, 3 - p, e_l).start()
            l_copy(8 * p + 2 * k + 1, 3 - p, e_r).start()
        else:
            r_copy(24 + k, 1, e_r).start()
            l_copy(24 + k, 1, e_l).start()

    def tick(p, forward):
        def body(k, u):
            ring_step(p, k)
            if forward is not None:
                for h in range(2):
                    i = 8 * p - 12 + 2 * k + h
                    x_recv(i)
                    forward(i)
            return u

        return body

    def forward(i):
        x_send(i, i + 8)

    def forward_last(i):
        @pl.when(c == lax.div(i - 16, 4))
        def _():
            x_send(i, 24 + lax.rem(i, 4))

    lax.fori_loop(0, 1, tick(1, None), 0)
    remote(z_mine, z_mine, s_zx, r_zx, z_there).wait_recv()
    remote(z_mine, z_mine, s_zp, r_zp, partner).start()
    x_own(4 + 2 * c)
    x_own(5 + 2 * c)
    lax.fori_loop(1, 2, tick(1, None), 0)
    remote(z_other, z_other, s_zp, r_zp, partner).wait_recv()
    x_own(4 + 2 * oc)
    x_own(5 + 2 * oc)
    lax.fori_loop(2, 4, tick(1, forward), 0)
    loads[3].wait()
    weights_block(x, first=True)
    lax.fori_loop(0, 2, tick(2, forward), 0)
    weights_block(_mod(x - sx))
    lax.fori_loop(2, 4, tick(2, forward), 0)
    partner_block(1)
    lax.fori_loop(0, 2, tick(3, forward), 0)
    weights_block(_mod(x - 2 * sx))
    lax.fori_loop(2, 4, tick(3, forward_last), 0)
    partner_block(2)

    far_first = (4, 3, 5, 2, 6, 1, 7)

    def last_step(k, u):
        r_copy(24 + k, 0, 0).wait_recv()
        part[pa, _mod(x + 4 - k)] += recv_r[24 + k]
        l_copy(24 + k, 0, 0).wait_recv()
        part[pa, _mod(x + k - 3)] += recv_l[24 + k]
        x_recv(20 + k)
        forward_last(20 + k)
        for e in far_first:
            for xx in (_mod(x + 4 - k), _mod(x + k - 3)):
                remote(part.at[pa, xx, _mod(pb + e)], recv2.at[e - 1, xx], s_2, r_2.at[e - 1], along_b(e)).start()
        return u

    lax.fori_loop(0, 4, last_step, 0)
    weights_block(_mod(x - 3 * sx))
    partner_block(3)
    for i in range(24, 28):
        x_recv(i)
    partner_block(4)
    weights_block(_mod(x + 4))
    vp_buf[...] = vp_acc[...].astype(jnp.bfloat16)
    vp_copy = pltpu.make_async_copy(vp_buf, vp_out, s_out.at[8])
    vp_copy.start()

    acc = part[pa, :, pb]
    for e in (1, 7, 2, 6, 3, 5, 4):
        here = recv2.at[e - 1]
        remote(here, here, s_2, r_2.at[e - 1], partner).wait_recv()
        acc += recv2[e - 1]
    s2_buf[:, 0] = acc[:, :4]
    s2_buf[:, 1] = acc[:, 4:]

    for e in far_first:
        for cc in range(2):
            xx = _mod(x + e)
            remote(s2_buf.at[xx, cc], recv3.at[c, e], s_3, r_3.at[c, e], dev(xx, y, z, cc)).start()
    remote(s2_buf.at[x, oc], recv3.at[c, 0], s_3, r_3.at[c, 0], partner).start()

    def got(from_core, e):
        here = recv3.at[from_core, e]
        remote(here, here, s_3, r_3.at[from_core, e], partner).wait_recv()
        return recv3[from_core, e]

    mine, theirs = s2_buf[x, c], got(oc, 0)
    for e in (1, 7, 2, 6, 3, 5, 4):
        mine += got(c, e)
        theirs += got(oc, e)
    mine, theirs = mine / scale, theirs / scale
    wg_buf[:, :256] = jnp.where(c == 0, mine, theirs)
    wg_buf[:, 256:] = jnp.where(c == 0, theirs, mine)
    wg_copy = pltpu.make_async_copy(wg_buf, wg_out, s_out.at[9])
    wg_copy.start()

    c_copy.wait_send()
    z_copy.wait_send()
    remote(z_mine, z_mine, s_zp, r_zp, partner).wait_send()
    mine = a_all.at[pl.ds(0, tok)]
    remote(mine, mine, s_ax, r_ax.at[0], partner).wait_send()
    for sem in (s_r, s_l, s_x, s_p):
        remote(recv_r, recv_r, sem, r_r.at[0], partner).wait_send()
    remote(recv2, recv2, s_2, r_2.at[0], partner).wait_send()
    for there in (recv3.at[0], recv3.at[1, pl.ds(0, 7)]):
        remote(there, there, s_3, r_3.at[0, 0], partner).wait_send()
    for b in range(8):
        at = pl.ds(b * cols, cols)
        pltpu.make_async_copy(ig_buf.at[:, at], ig_out.at[:, at], s_out.at[b]).wait()
    vp_copy.wait()
    wg_copy.wait()


def per_device(activations, value_weight, value_cotangent):
    tok, d = activations.shape
    rows, v = value_weight.shape
    tokens = tok * lax.axis_size("dp") * lax.axis_size("tensor")
    f32, bf16 = jnp.float32, jnp.bfloat16
    dma, vm = pltpu.SemaphoreType.DMA, pltpu.VMEM
    hbm = pl.BlockSpec(memory_space=pl.ANY)
    return pl.pallas_call(
        functools.partial(_kernel, float(tokens) ** 0.5),
        out_shape=(
            jax.ShapeDtypeStruct((tok, v), bf16),
            jax.ShapeDtypeStruct((tok, d), bf16),
            jax.ShapeDtypeStruct((rows * lax.axis_size("tensor") // 1024, v), f32),
        ),
        in_specs=[pl.BlockSpec(memory_space=pltpu.HBM)] * 3,
        out_specs=(hbm,) * 3,
        scratch_shapes=[
            vm((256, 4096), bf16), vm((256, 256), bf16), vm((128, 512), bf16), vm((8, 8, 64, 512), bf16),
            vm((8, 8, 8, 8, 256), f32), vm((ITEMS, 8, 8, 256), f32), vm((ITEMS, 8, 8, 256), f32),
            vm((7, 8, 8, 256), f32), vm((8, 2, 4, 256), f32), vm((2, 8, 4, 256), f32),
            vm((128, 512), f32), vm((128, 512), bf16), vm((128, 4096), bf16), vm((4, 512), f32),
            dma((4,)), dma, dma((8,)), dma, dma, dma, dma, dma, dma,
            dma, dma((ITEMS,)), dma, dma((ITEMS,)), dma, dma((ITEMS,)), dma, dma((4,)),
            dma, dma((7,)), dma, dma((2, 8)), dma((10,)),
        ],
        compiler_params=pltpu.CompilerParams(
            collective_id=0, has_side_effects=True, vmem_limit_bytes=48 * 1024 * 1024
        ),
    )(*(pltpu.with_memory_space_constraint(a, pltpu.HBM) for a in (activations, value_weight.reshape(4, 64, v), value_cotangent)))


def solution(mesh):
    placed = (P(("dp", "tensor"), None), P("tensor", None), P(("dp", "tensor"), None))
    return jax.shard_map(
        per_device,
        mesh=mesh,
        in_specs=placed,
        out_specs=(P(("dp", "tensor"), None), P(("dp", "tensor"), None), P(("tensor", "dp"), None)),
        check_vma=False,
    )
```

```python
import functools

import jax
import jax.numpy as jnp
from jax import lax
from jax.experimental import pallas as pl
from jax.experimental.pallas import tpu as pltpu
from jax.sharding import PartitionSpec as P

MESH = pl.DeviceIdType.MESH
RING = 8
ITEMS = 28


def _mod(v):
    return lax.rem(v + 4 * RING, RING)


def _kernel(scale, acts, w, cot, vp_out, ig_out, wg_out,
            a_all, c_pair, c_own, w_all, part, recv_r, recv_l, recv2, s2_buf, recv3,
            vp_acc, vp_buf, ig_buf, wg_buf,
            s_load, s_ax, r_ax, s_cx, r_cx, s_zx, r_zx, s_zp, r_zp,
            s_r, r_r, s_l, r_l, s_x, r_x, s_p, r_p, s_2, r_2, s_3, r_3, s_out):
    dp, tn = lax.axis_index("dp"), lax.axis_index("tensor")
    c, y, zh = lax.rem(dp, 2), lax.rem(lax.div(dp, 2), RING), lax.div(dp, 2 * RING)
    x, zl = lax.div(tn, 2), lax.rem(tn, 2)
    z = zh * 2 + zl
    oc = 1 - c
    sx = 1 - 2 * c
    pa = y * oc + z * c
    pb = z * oc + y * c

    def dev(xx, yy, zz, cc):
        return {"dp": lax.div(zz, 2) * (2 * RING) + yy * 2 + cc, "tensor": xx * 2 + lax.rem(zz, 2)}

    def along_a(step):
        return dev(x, _mod(y + step * oc), _mod(z + step * c), c)

    def along_b(step):
        return dev(x, _mod(y + step * c), _mod(z + step * oc), c)

    def along_x(step):
        return dev(_mod(x + step), y, z, c)

    partner = dev(x, y, z, oc)
    tok, cols = 128, 512

    barrier = pltpu.get_barrier_semaphore()
    for there in (partner, along_a(1), along_a(-1), along_b(1), along_b(-1), along_x(1), along_x(-1)):
        pl.semaphore_signal(barrier, inc=1, device_id=there, device_id_type=MESH)

    loads = [
        pltpu.make_async_copy(acts, a_all.at[pl.ds(0, tok)], s_load.at[0]),
        pltpu.make_async_copy(cot.at[:, pl.ds(pl.multiple_of(c * 256, 256), 256)], c_pair.at[pl.ds(0, tok)], s_load.at[1]),
        pltpu.make_async_copy(cot, c_own, s_load.at[2]),
        pltpu.make_async_copy(w, w_all.at[x, pl.ds(zl * 4, 4)], s_load.at[3]),
    ]
    for load in loads:
        load.start()
    pl.semaphore_wait(barrier, 7)

    def remote(src, dst, send, recv, there):
        return pltpu.make_async_remote_copy(
            src_ref=src, dst_ref=dst, send_sem=send, recv_sem=recv, device_id=there, device_id_type=MESH
        )

    z_there = dev(x, y, _mod(z - sx), c)
    z_copy = remote(w.at[pl.ds(2 * c, 2)], w_all.at[x, pl.ds(zl * 4 + 2 * c, 2)], s_zx, r_zx, z_there)
    z_copy.start()
    z_mine = w_all.at[x, pl.ds((1 - zl) * 4 + 2 * c, 2)]
    z_other = w_all.at[x, pl.ds((1 - zl) * 4 + 2 * oc, 2)]

    def order(j):
        k = j // 2
        return 4 - k if j % 2 == 0 else k - 3

    def a_copy(j):
        block = pl.ds(pl.multiple_of(_mod(x + order(j)) * cols, cols), cols)
        return remote(acts.at[:, block], a_all.at[pl.ds(tok, tok), block], s_ax, r_ax.at[j], partner)

    c_copy = remote(cot.at[:, pl.ds(pl.multiple_of(oc * 256, 256), 256)], c_pair.at[pl.ds(tok, tok)], s_cx, r_cx, partner)
    c_copy.start()
    for j in range(8):
        a_copy(j).start()

    def unit(m):
        return lax.rem(zl + m // 4, 2) * 4 + lax.rem(m, 4)

    x_there = along_x(sx)

    def x_in(i):
        m = lax.rem(i, 8) + lax.div(i, 24) * 4 * c
        return w_all.at[_mod(x - sx * (i // 8 + 1)), unit(m)]

    def x_recv(i):
        here = x_in(i)
        remote(here, here, s_x, r_x.at[i], x_there).wait_recv()
        remote(here, here, s_p, r_p.at[i // 8], partner).start()

    def x_send(i, out):
        here = x_in(i)
        remote(here, here, s_x, r_x.at[out], x_there).start()

    def x_own(m):
        here = w_all.at[x, unit(m)]
        remote(here, here, s_x, r_x.at[m], x_there).start()

    for m in range(4):
        remote(w.at[m], w_all.at[x, unit(m)], s_x, r_x.at[m], x_there).start()

    def weights_block(block, first=False):
        at = pl.ds(pl.multiple_of(block * cols, cols), cols)
        wb = w_all[block].reshape(cols, cols)
        term = jnp.dot(a_all[pl.ds(0, tok), at], wb, preferred_element_type=jnp.float32)
        if first:
            vp_acc[...] = term
        else:
            vp_acc[...] += term
        grad = lax.dot_general(c_own[...], wb, (((1,), (1,)), ((), ())), preferred_element_type=jnp.float32)
        ig_buf[:, at] = grad.astype(jnp.bfloat16)
        pltpu.make_async_copy(ig_buf.at[:, at], ig_out.at[:, at], s_out.at[block]).start()

    def partner_block(p):
        whole = w_all.at[0] if p < 4 else w_all.at[0, pl.ds(0, 4)]
        remote(whole, whole, s_p, r_p.at[p - 1], partner).wait_recv()
        if p < 4:
            weights_block(_mod(x + sx * p))

    right, left = along_a(1), along_a(-1)

    def r_copy(n, to, xx):
        return remote(part.at[_mod(pa + to), _mod(x + xx)], recv_r.at[n], s_r, r_r.at[n], right)

    def l_copy(n, to, xx):
        return remote(part.at[_mod(pa - to), _mod(x + xx)], recv_l.at[n], s_l, r_l.at[n], left)

    for load in loads[:3]:
        load.wait()
    c_copy.wait_recv()
    for j in range(8):
        k = j // 2
        a_copy(j).wait_recv()
        xb = _mod(x + order(j))
        at = pl.ds(pl.multiple_of(xb * cols, cols), cols)
        prod = lax.dot_general(
            a_all[:, at], c_pair[...], (((0,), (0,)), ((), ())), preferred_element_type=jnp.float32
        )
        for zz in range(8):
            base = (zz % 2) * 256 + (zz // 2) * 64
            for yy in range(8):
                part[yy * oc + zz * c, xb, zz * oc + yy * c] = prod[base + yy * 8 : base + yy * 8 + 8]
        if j % 2 == 0:
            r_copy(2 * k, 4, order(j)).start()
            l_copy(2 * k + 1, 3, order(j)).start()
        else:
            r_copy(2 * k + 1, 3, order(j)).start()
            l_copy(2 * k, 4, order(j)).start()

    remote(z_mine, z_mine, s_zx, r_zx, z_there).wait_recv()
    remote(z_mine, z_mine, s_zp, r_zp, partner).start()
    x_own(4 + 2 * c)
    x_own(5 + 2 * c)

    orders = (
        ((0, 0), (1, 0), (0, 1), (1, 1), (0, 2), (1, 2), (0, 3), (1, 3)),
        ((0, 0), (0, 1), (1, 0), (0, 2), (1, 1), (0, 3), (1, 2), (1, 3)),
        ((0, 0), (0, 1), (0, 2), (0, 3), (1, 0), (1, 1), (1, 2), (1, 3)),
        ((0, 0), (0, 1), (0, 2), (0, 3)),
    )

    def ring_step(p, pieces):
        for odd, k in pieces:
            n = 8 * (p - 1) + orders[p - 1].index((odd, k))
            to = 4 - p - odd
            e_r, e_l = (k - 3, 4 - k) if odd else (4 - k, k - 3)
            r_copy(n, 0, 0).wait_recv()
            part[_mod(pa + to), _mod(x + e_r)] += recv_r[n]
            l_copy(n, 0, 0).wait_recv()
            part[_mod(pa - to), _mod(x + e_l)] += recv_l[n]
        for odd, k in pieces:
            to = 4 - p - odd
            e_r, e_l = (k - 3, 4 - k) if odd else (4 - k, k - 3)
            if to > 0:
                n = 8 * p + orders[p].index((odd, k))
                r_copy(n, to, e_r).start()
                l_copy(n, to, e_l).start()

    def pass_on(i):
        x_recv(i)
        if i < 16:
            x_send(i, i + 8)
        elif i < 24:

            @pl.when(c == i // 4 - 4)
            def _():
                x_send(i, 24 + i % 4)

    for p in (1, 2, 3):
        pieces = orders[min(p, 2)]
        for t in range(4):
            ring_step(p, pieces[2 * t : 2 * t + 2])
            if p == 1 and t == 0:
                remote(z_other, z_other, s_zp, r_zp, partner).wait_recv()
                x_own(4 + 2 * oc)
                x_own(5 + 2 * oc)
            for i in (8 * p - 10 + 2 * t, 8 * p - 9 + 2 * t):
                if i >= 0:
                    pass_on(i)
            if t == 1 and p > 1:
                weights_block(_mod(x - (p - 1) * sx))
            if t == 3 and p == 1:
                loads[3].wait()
                weights_block(x, first=True)
            if t == 3 and p > 1:
                partner_block(p - 1)

    far_first = (4, 3, 5, 2, 6, 1, 7)

    for k in range(4):
        r_copy(24 + k, 0, 0).wait_recv()
        part[pa, _mod(x + 4 - k)] += recv_r[24 + k]
        l_copy(24 + k, 0, 0).wait_recv()
        part[pa, _mod(x + k - 3)] += recv_l[24 + k]
        for b in range(RING):

            @pl.when(pb != b)
            def _():
                e = _mod(b - pb) - 1
                for xx in (_mod(x + 4 - k), _mod(x + k - 3)):
                    remote(part.at[pa, xx, b], recv2.at[e, xx], s_2, r_2.at[e], along_b(e + 1)).start()

        if k < 2:
            pass_on(22 + k)

    weights_block(_mod(x - 3 * sx))
    partner_block(3)
    for i in range(24, 28):
        x_recv(i)
    partner_block(4)
    weights_block(_mod(x + 4))
    vp_buf[...] = vp_acc[...].astype(jnp.bfloat16)
    vp_copy = pltpu.make_async_copy(vp_buf, vp_out, s_out.at[8])
    vp_copy.start()

    acc = part[pa, :, pb]
    for e in (1, 7, 2, 6, 3, 5, 4):
        here = recv2.at[e - 1]
        remote(here, here, s_2, r_2.at[e - 1], partner).wait_recv()
        acc += recv2[e - 1]
    s2_buf[:, 0] = acc[:, :4]
    s2_buf[:, 1] = acc[:, 4:]

    for e in far_first:
        for cc in range(2):
            xx = _mod(x + e)
            remote(s2_buf.at[xx, cc], recv3.at[c, e], s_3, r_3.at[c, e], dev(xx, y, z, cc)).start()
    remote(s2_buf.at[x, oc], recv3.at[c, 0], s_3, r_3.at[c, 0], partner).start()

    def got(from_core, e):
        here = recv3.at[from_core, e]
        remote(here, here, s_3, r_3.at[from_core, e], partner).wait_recv()
        return recv3[from_core, e]

    mine, theirs = s2_buf[x, c], got(oc, 0)
    for e in (1, 7, 2, 6, 3, 5, 4):
        mine += got(c, e)
        theirs += got(oc, e)
    mine, theirs = mine / scale, theirs / scale
    wg_buf[:, :256] = jnp.where(c == 0, mine, theirs)
    wg_buf[:, 256:] = jnp.where(c == 0, theirs, mine)
    wg_copy = pltpu.make_async_copy(wg_buf, wg_out, s_out.at[9])
    wg_copy.start()

    c_copy.wait_send()
    z_copy.wait_send()
    remote(z_mine, z_mine, s_zp, r_zp, partner).wait_send()
    mine = a_all.at[pl.ds(0, tok)]
    remote(mine, mine, s_ax, r_ax.at[0], partner).wait_send()
    for sem in (s_r, s_l, s_x, s_p):
        remote(recv_r, recv_r, sem, r_r.at[0], partner).wait_send()
    remote(recv2, recv2, s_2, r_2.at[0], partner).wait_send()
    for there in (recv3.at[0], recv3.at[1, pl.ds(0, 7)]):
        remote(there, there, s_3, r_3.at[0, 0], partner).wait_send()
    for b in range(8):
        at = pl.ds(b * cols, cols)
        pltpu.make_async_copy(ig_buf.at[:, at], ig_out.at[:, at], s_out.at[b]).wait()
    vp_copy.wait()
    wg_copy.wait()


def _store(vp, ig, wg, vp_out, ig_out, wg_out, sem):
    rows = ig.shape[0] // 4
    copies = [pltpu.make_async_copy(ig.at[pl.ds(i * rows, rows)], ig_out.at[pl.ds(i * rows, rows)], sem.at[i]) for i in range(4)]
    copies += [pltpu.make_async_copy(vp, vp_out, sem.at[4]), pltpu.make_async_copy(wg, wg_out, sem.at[5])]
    for copy in copies:
        copy.start()
    for copy in copies:
        copy.wait()


def per_device(activations, value_weight, value_cotangent):
    tok, d = activations.shape
    rows, v = value_weight.shape
    tokens = tok * lax.axis_size("dp") * lax.axis_size("tensor")
    f32, bf16 = jnp.float32, jnp.bfloat16
    dma, vm = pltpu.SemaphoreType.DMA, pltpu.VMEM
    hbm = pl.BlockSpec(memory_space=pl.ANY)
    shapes = (
        jax.ShapeDtypeStruct((tok, v), bf16),
        jax.ShapeDtypeStruct((tok, d), bf16),
        jax.ShapeDtypeStruct((rows * lax.axis_size("tensor") // 1024, v), f32),
    )
    results = pl.pallas_call(
        functools.partial(_kernel, float(tokens) ** 0.5),
        out_shape=shapes,
        in_specs=[pl.BlockSpec(memory_space=pltpu.HBM)] * 3,
        out_specs=(hbm,) * 3,
        scratch_shapes=[
            vm((256, 4096), bf16), vm((256, 256), bf16), vm((128, 512), bf16), vm((8, 8, 64, 512), bf16),
            vm((8, 8, 8, 8, 256), f32), vm((ITEMS, 8, 8, 256), f32), vm((ITEMS, 8, 8, 256), f32),
            vm((7, 8, 8, 256), f32), vm((8, 2, 4, 256), f32), vm((2, 8, 4, 256), f32),
            vm((128, 512), f32), vm((128, 512), bf16), vm((128, 4096), bf16), vm((4, 512), f32),
            dma((4,)), dma, dma((8,)), dma, dma, dma, dma, dma, dma,
            dma, dma((ITEMS,)), dma, dma((ITEMS,)), dma, dma((ITEMS,)), dma, dma((4,)),
            dma, dma((7,)), dma, dma((2, 8)), dma((10,)),
        ],
        compiler_params=pltpu.CompilerParams(
            collective_id=0, has_side_effects=True, vmem_limit_bytes=48 * 1024 * 1024
        ),
    )(*(pltpu.with_memory_space_constraint(a, pltpu.HBM) for a in (activations, value_weight.reshape(4, 64, v), value_cotangent)))
    return pl.pallas_call(
        _store, out_shape=shapes, in_specs=[hbm] * 3, out_specs=(hbm,) * 3, scratch_shapes=[dma((6,))],
        compiler_params=pltpu.CompilerParams(vmem_limit_bytes=1024 * 1024),
    )(*results)


def solution(mesh):
    placed = (P(("dp", "tensor"), None), P("tensor", None), P(("dp", "tensor"), None))
    return jax.shard_map(
        per_device,
        mesh=mesh,
        in_specs=placed,
        out_specs=(P(("dp", "tensor"), None), P(("dp", "tensor"), None), P(("tensor", "dp"), None)),
        check_vma=False,
    )
```

```python
import functools

import jax
import jax.numpy as jnp
from jax import lax
from jax.experimental import pallas as pl
from jax.experimental.pallas import tpu as pltpu
from jax.sharding import PartitionSpec as P

MESH = pl.DeviceIdType.MESH
RING = 8
ITEMS = 28


def _mod(v):
    return lax.rem(v + 4 * RING, RING)


def _kernel(scale, acts, w, cot, vp_out, ig_out, wg_out,
            a_all, c_pair, c_own, w_all, part, recv_r, recv_l, recv2, s2_buf, recv3,
            recvx_r, recvx_l, recv4, v_buf, recv5,
            vp_acc, vp_buf, ig_buf, wg_buf,
            s_load, s_ax, r_ax, s_cx, r_cx, s_zx, r_zx, s_zp, r_zp,
            s_r, r_r, s_l, r_l, s_x, r_x, s_p, r_p, s_2, r_2, s_3, r_3,
            s_xr, r_xr, s_xl, r_xl, s_4, r_4, s_5, r_5, s_out):
    dp, tn = lax.axis_index("dp"), lax.axis_index("tensor")
    c, y, zh = lax.rem(dp, 2), lax.rem(lax.div(dp, 2), RING), lax.div(dp, 2 * RING)
    x, zl = lax.div(tn, 2), lax.rem(tn, 2)
    z = zh * 2 + zl
    oc = 1 - c
    sx = 1 - 2 * c
    pa = y * oc + z * c
    pb = z * oc + y * c

    def dev(xx, yy, zz, cc):
        return {"dp": lax.div(zz, 2) * (2 * RING) + yy * 2 + cc, "tensor": xx * 2 + lax.rem(zz, 2)}

    def along_a(step):
        return dev(x, _mod(y + step * oc), _mod(z + step * c), c)

    def along_b(step, core=None):
        return dev(x, _mod(y + step * c), _mod(z + step * oc), c if core is None else core)

    def along_x(step):
        return dev(_mod(x + step), y, z, c)

    partner = dev(x, y, z, oc)
    tok, cols = 128, 512

    barrier = pltpu.get_barrier_semaphore()
    for there in (partner, along_a(1), along_a(-1), along_b(1), along_b(-1), along_x(1), along_x(-1)):
        pl.semaphore_signal(barrier, inc=1, device_id=there, device_id_type=MESH)

    loads = [
        pltpu.make_async_copy(acts, a_all.at[pl.ds(0, tok)], s_load.at[0]),
        pltpu.make_async_copy(cot.at[:, pl.ds(pl.multiple_of(c * 256, 256), 256)], c_pair.at[pl.ds(0, tok)], s_load.at[1]),
        pltpu.make_async_copy(cot, c_own, s_load.at[2]),
        pltpu.make_async_copy(w, w_all.at[x, pl.ds(zl * 4, 4)], s_load.at[3]),
    ]
    for load in loads:
        load.start()
    pl.semaphore_wait(barrier, 7)

    def remote(src, dst, send, recv, there):
        return pltpu.make_async_remote_copy(
            src_ref=src, dst_ref=dst, send_sem=send, recv_sem=recv, device_id=there, device_id_type=MESH
        )

    z_there = dev(x, y, _mod(z - sx), c)
    z_copy = remote(w.at[pl.ds(2 * c, 2)], w_all.at[x, pl.ds(zl * 4 + 2 * c, 2)], s_zx, r_zx, z_there)
    z_copy.start()
    z_mine = w_all.at[x, pl.ds((1 - zl) * 4 + 2 * c, 2)]
    z_other = w_all.at[x, pl.ds((1 - zl) * 4 + 2 * oc, 2)]

    def order(j):
        k = j // 2
        return 4 - k if j % 2 == 0 else k - 3

    def a_copy(j):
        block = pl.ds(pl.multiple_of(_mod(x + order(j)) * cols, cols), cols)
        return remote(acts.at[:, block], a_all.at[pl.ds(tok, tok), block], s_ax, r_ax.at[j], partner)

    c_copy = remote(cot.at[:, pl.ds(pl.multiple_of(oc * 256, 256), 256)], c_pair.at[pl.ds(tok, tok)], s_cx, r_cx, partner)
    c_copy.start()
    for j in range(8):
        a_copy(j).start()

    def unit(m):
        return lax.rem(zl + m // 4, 2) * 4 + lax.rem(m, 4)

    x_there = along_x(sx)

    def x_in(i):
        m = lax.rem(i, 8) + lax.div(i, 24) * 4 * c
        return w_all.at[_mod(x - sx * (i // 8 + 1)), unit(m)]

    def x_recv(i):
        here = x_in(i)
        remote(here, here, s_x, r_x.at[i], x_there).wait_recv()
        remote(here, here, s_p, r_p.at[i // 8], partner).start()

    def x_send(i, out):
        here = x_in(i)
        remote(here, here, s_x, r_x.at[out], x_there).start()

    def x_own(m):
        here = w_all.at[x, unit(m)]
        remote(here, here, s_x, r_x.at[m], x_there).start()

    for m in range(4):
        remote(w.at[m], w_all.at[x, unit(m)], s_x, r_x.at[m], x_there).start()

    def weights_block(block, first=False):
        at = pl.ds(pl.multiple_of(block * cols, cols), cols)
        wb = w_all[block].reshape(cols, cols)
        term = jnp.dot(a_all[pl.ds(0, tok), at], wb, preferred_element_type=jnp.float32)
        if first:
            vp_acc[...] = term
        else:
            vp_acc[...] += term
        grad = lax.dot_general(c_own[...], wb, (((1,), (1,)), ((), ())), preferred_element_type=jnp.float32)
        ig_buf[:, at] = grad.astype(jnp.bfloat16)
        pltpu.make_async_copy(ig_buf.at[:, at], ig_out.at[:, at], s_out.at[block]).start()

    def partner_block(p):
        whole = w_all.at[0] if p < 4 else w_all.at[0, pl.ds(0, 4)]
        remote(whole, whole, s_p, r_p.at[p - 1], partner).wait_recv()
        if p < 4:
            weights_block(_mod(x + sx * p))

    right, left = along_a(1), along_a(-1)
    near, far = pl.ds(0, 7), 7
    slots = [_mod(v - pb + 3) for v in range(8)]
    x_right, x_left = along_x(1), along_x(-1)

    def xr_copy(n):
        src = part.at[pl.ds(n % 2 * 4, 4), _mod(x + 4 - (n + 1) // 2), far]
        return remote(src, recvx_r.at[n], s_xr, r_xr.at[n], x_right)

    def xl_copy(n):
        src = part.at[pl.ds((n + 1) % 2 * 4, 4), _mod(x - 4 + (n + 1) // 2), far]
        return remote(src, recvx_l.at[n], s_xl, r_xl.at[n], x_left)

    def x_step(items):
        for n in items:
            to = 3 - (n + 1) // 2
            xr_copy(n).wait_recv()
            part[n % 2 * 4 : n % 2 * 4 + 4, _mod(x + to), far] += recvx_r[n]
            h = (n + 1) % 2 * 4
            xl_copy(n).wait_recv()
            part[h : h + 4, _mod(x - to), far] += recvx_l[n]
        for n in items:
            if n + 2 < 7:
                xr_copy(n + 2).start()
                xl_copy(n + 2).start()

    def r_copy(n, to, xx):
        return remote(part.at[_mod(pa + to), _mod(x + xx), near], recv_r.at[n], s_r, r_r.at[n], right)

    def l_copy(n, to, xx):
        return remote(part.at[_mod(pa - to), _mod(x + xx), near], recv_l.at[n], s_l, r_l.at[n], left)

    for load in loads[:3]:
        load.wait()
    c_copy.wait_recv()
    for j in range(8):
        k = j // 2
        a_copy(j).wait_recv()
        xb = _mod(x + order(j))
        at = pl.ds(pl.multiple_of(xb * cols, cols), cols)
        prod = lax.dot_general(
            a_all[:, at], c_pair[...], (((0,), (0,)), ((), ())), preferred_element_type=jnp.float32
        )
        for zz in range(8):
            base = (zz % 2) * 256 + (zz // 2) * 64
            for yy in range(8):
                part[yy * oc + zz * c, xb, slots[zz] * oc + slots[yy] * c] = prod[base + yy * 8 : base + yy * 8 + 8]
        if j % 2 == 0:
            r_copy(2 * k, 4, order(j)).start()
            l_copy(2 * k + 1, 3, order(j)).start()
        else:
            r_copy(2 * k + 1, 3, order(j)).start()
            l_copy(2 * k, 4, order(j)).start()
        if j in (0, 2):
            xr_copy(j // 2).start()
            xl_copy(j // 2).start()

    remote(z_mine, z_mine, s_zx, r_zx, z_there).wait_recv()
    remote(z_mine, z_mine, s_zp, r_zp, partner).start()
    x_own(4 + 2 * c)
    x_own(5 + 2 * c)

    orders = (
        ((0, 0), (1, 0), (0, 1), (1, 1), (0, 2), (1, 2), (0, 3), (1, 3)),
        ((0, 0), (0, 1), (1, 0), (0, 2), (1, 1), (0, 3), (1, 2), (1, 3)),
        ((0, 0), (0, 1), (0, 2), (0, 3), (1, 0), (1, 1), (1, 2), (1, 3)),
        ((0, 0), (0, 1), (0, 2), (0, 3)),
    )

    def ring_step(p, pieces):
        for odd, k in pieces:
            n = 8 * (p - 1) + orders[p - 1].index((odd, k))
            to = 4 - p - odd
            e_r, e_l = (k - 3, 4 - k) if odd else (4 - k, k - 3)
            r_copy(n, 0, 0).wait_recv()
            part[_mod(pa + to), _mod(x + e_r), 0:7] += recv_r[n]
            l_copy(n, 0, 0).wait_recv()
            part[_mod(pa - to), _mod(x + e_l), 0:7] += recv_l[n]
        for odd, k in pieces:
            to = 4 - p - odd
            e_r, e_l = (k - 3, 4 - k) if odd else (4 - k, k - 3)
            if to > 0:
                n = 8 * p + orders[p].index((odd, k))
                r_copy(n, to, e_r).start()
                l_copy(n, to, e_l).start()

    def pass_on(i):
        x_recv(i)
        if i < 16:
            x_send(i, i + 8)
        elif i < 24:

            @pl.when(c == i // 4 - 4)
            def _():
                x_send(i, 24 + i % 4)

    for p in (1, 2, 3):
        pieces = orders[min(p, 2)]
        for t in range(4):
            ring_step(p, pieces[2 * t : 2 * t + 2])
            if p == 1 and t == 0:
                remote(z_other, z_other, s_zp, r_zp, partner).wait_recv()
                x_own(4 + 2 * oc)
                x_own(5 + 2 * oc)
            for i in (8 * p - 12 + 2 * t, 8 * p - 11 + 2 * t):
                if i >= 0:
                    pass_on(i)
            if t == 1:
                x_step((2 * p - 2, 2 * p - 1))
            if t == 1 and p > 1:
                weights_block(_mod(x - (p - 1) * sx))
            if t == 3 and p == 1:
                loads[3].wait()
                weights_block(x, first=True)
            if t == 3 and p > 1:
                partner_block(p - 1)

    far_first = (4, 3, 5, 2, 6, 1, 7)

    for k in range(4):
        r_copy(24 + k, 0, 0).wait_recv()
        part[pa, _mod(x + 4 - k), 0:7] += recv_r[24 + k]
        l_copy(24 + k, 0, 0).wait_recv()
        part[pa, _mod(x + k - 3), 0:7] += recv_l[24 + k]
        for e in (3, -3, 2, -2, 1, -1):
            for xx in (_mod(x + 4 - k), _mod(x + k - 3)):
                remote(part.at[pa, xx, e + 3], recv2.at[e + 3, xx], s_2, r_2.at[e + 3], along_b(e)).start()
        pass_on(20 + k)

    x_step((6,))
    for e in far_first:
        remote(part.at[_mod(pa + e), x, far], recv4.at[e - 1], s_4, r_4.at[e - 1], along_a(e)).start()
    weights_block(_mod(x - 3 * sx))
    val = part[pa, x, far]
    for e in (1, 7, 2, 6, 3, 5, 4):
        here = recv4.at[e - 1]
        remote(here, here, s_4, r_4.at[e - 1], partner).wait_recv()
        val += recv4[e - 1]
    v_buf[0] = val[:4]
    v_buf[1] = val[4:]
    for cc in range(2):
        remote(v_buf.at[cc], recv5.at[c], s_5, r_5.at[c], along_b(4, cc)).start()

    acc = part[pa, :, 3]
    for e in (-1, 1, -2, 2, -3, 3):
        here = recv2.at[e + 3]
        remote(here, here, s_2, r_2.at[e + 3], partner).wait_recv()
        acc += recv2[e + 3]
    s2_buf[:, 0] = acc[:, :4]
    s2_buf[:, 1] = acc[:, 4:]

    for e in far_first:
        for cc in range(2):
            xx = _mod(x + e)
            remote(s2_buf.at[xx, cc], recv3.at[c, e], s_3, r_3.at[c, e], dev(xx, y, z, cc)).start()
    remote(s2_buf.at[x, oc], recv3.at[c, 0], s_3, r_3.at[c, 0], partner).start()

    partner_block(3)
    for i in range(24, 28):
        x_recv(i)
    partner_block(4)
    weights_block(_mod(x + 4))
    vp_buf[...] = vp_acc[...].astype(jnp.bfloat16)
    vp_copy = pltpu.make_async_copy(vp_buf, vp_out, s_out.at[8])
    vp_copy.start()

    def got(from_core, e):
        here = recv3.at[from_core, e]
        remote(here, here, s_3, r_3.at[from_core, e], partner).wait_recv()
        return recv3[from_core, e]

    mine, theirs = s2_buf[x, c], got(oc, 0)
    for e in (1, 7, 2, 6, 3, 5, 4):
        mine += got(c, e)
        theirs += got(oc, e)
    for core in range(2):
        here = recv5.at[core]
        remote(here, here, s_5, r_5.at[core], partner).wait_recv()
    mine, theirs = (mine + recv5[c]) / scale, (theirs + recv5[oc]) / scale
    wg_buf[:, :256] = jnp.where(c == 0, mine, theirs)
    wg_buf[:, 256:] = jnp.where(c == 0, theirs, mine)
    wg_copy = pltpu.make_async_copy(wg_buf, wg_out, s_out.at[9])
    wg_copy.start()

    c_copy.wait_send()
    z_copy.wait_send()
    remote(z_mine, z_mine, s_zp, r_zp, partner).wait_send()
    mine = a_all.at[pl.ds(0, tok)]
    remote(mine, mine, s_ax, r_ax.at[0], partner).wait_send()
    for sem in (s_r, s_l):
        remote(recv_r, recv_r, sem, r_r.at[0], partner).wait_send()
    for sem in (s_x, s_p):
        for there in (w_all.at[pl.ds(0, 3)], w_all.at[0, pl.ds(0, 4)]):
            remote(there, there, sem, r_r.at[0], partner).wait_send()
    for there, sem in ((recv2.at[pl.ds(0, 6)], s_2), (recvx_r, s_xr), (recvx_l, s_xl), (recv4, s_4), (recv5, s_5)):
        remote(there, there, sem, r_r.at[0], partner).wait_send()
    for there in (recv3.at[0], recv3.at[1, pl.ds(0, 7)]):
        remote(there, there, s_3, r_3.at[0, 0], partner).wait_send()
    for b in range(8):
        at = pl.ds(b * cols, cols)
        pltpu.make_async_copy(ig_buf.at[:, at], ig_out.at[:, at], s_out.at[b]).wait()
    vp_copy.wait()
    wg_copy.wait()


def _store(vp, ig, wg, vp_out, ig_out, wg_out, sem):
    rows = ig.shape[0] // 4
    copies = [pltpu.make_async_copy(ig.at[pl.ds(i * rows, rows)], ig_out.at[pl.ds(i * rows, rows)], sem.at[i]) for i in range(4)]
    copies += [pltpu.make_async_copy(vp, vp_out, sem.at[4]), pltpu.make_async_copy(wg, wg_out, sem.at[5])]
    for copy in copies:
        copy.start()
    for copy in copies:
        copy.wait()


def per_device(activations, value_weight, value_cotangent):
    tok, d = activations.shape
    rows, v = value_weight.shape
    tokens = tok * lax.axis_size("dp") * lax.axis_size("tensor")
    f32, bf16 = jnp.float32, jnp.bfloat16
    dma, vm = pltpu.SemaphoreType.DMA, pltpu.VMEM
    hbm = pl.BlockSpec(memory_space=pl.ANY)
    shapes = (
        jax.ShapeDtypeStruct((tok, v), bf16),
        jax.ShapeDtypeStruct((tok, d), bf16),
        jax.ShapeDtypeStruct((rows * lax.axis_size("tensor") // 1024, v), f32),
    )
    results = pl.pallas_call(
        functools.partial(_kernel, float(tokens) ** 0.5),
        out_shape=shapes,
        in_specs=[pl.BlockSpec(memory_space=pltpu.HBM)] * 3,
        out_specs=(hbm,) * 3,
        scratch_shapes=[
            vm((256, 4096), bf16), vm((256, 256), bf16), vm((128, 512), bf16), vm((8, 8, 64, 512), bf16),
            vm((8, 8, 8, 8, 256), f32), vm((ITEMS, 7, 8, 256), f32), vm((ITEMS, 7, 8, 256), f32),
            vm((7, 8, 8, 256), f32), vm((8, 2, 4, 256), f32), vm((2, 8, 4, 256), f32),
            vm((7, 4, 8, 256), f32), vm((7, 4, 8, 256), f32), vm((7, 8, 256), f32), vm((2, 4, 256), f32), vm((2, 4, 256), f32),
            vm((128, 512), f32), vm((128, 512), bf16), vm((128, 4096), bf16), vm((4, 512), f32),
            dma((4,)), dma, dma((8,)), dma, dma, dma, dma, dma, dma,
            dma, dma((ITEMS,)), dma, dma((ITEMS,)), dma, dma((ITEMS,)), dma, dma((4,)),
            dma, dma((7,)), dma, dma((2, 8)),
            dma, dma((7,)), dma, dma((7,)), dma, dma((7,)), dma, dma((2,)), dma((10,)),
        ],
        compiler_params=pltpu.CompilerParams(
            collective_id=0, has_side_effects=True, vmem_limit_bytes=48 * 1024 * 1024
        ),
    )(*(pltpu.with_memory_space_constraint(a, pltpu.HBM) for a in (activations, value_weight.reshape(4, 64, v), value_cotangent)))
    return pl.pallas_call(
        _store, out_shape=shapes, in_specs=[hbm] * 3, out_specs=(hbm,) * 3, scratch_shapes=[dma((6,))],
        compiler_params=pltpu.CompilerParams(vmem_limit_bytes=1024 * 1024),
    )(*results)


def solution(mesh):
    placed = (P(("dp", "tensor"), None), P("tensor", None), P(("dp", "tensor"), None))
    return jax.shard_map(
        per_device,
        mesh=mesh,
        in_specs=placed,
        out_specs=(P(("dp", "tensor"), None), P(("dp", "tensor"), None), P(("tensor", "dp"), None)),
        check_vma=False,
    )
```
